256 devices in a mesh: shuf: 4 (over y_lo, core), key: 64 (over x, z, y_hi).
Axes of the slice: x: 4, y: 4 (y_hi: 2, y_lo: 2; y = y_hi * 2 + y_lo), z: 8, core: 2. Of those that a mesh axis runs over, the one named last changes fastest.
Arguments:
- embeddings: bfloat16 [32768, 1024], P(('shuf', 'key')), may hold values from -200 to 200
- labels: int32 [32768], P(('shuf', 'key')), may hold values from 0 to 2047
- order: int32 [256, 128], P(('shuf', 'key')), may hold values from 0 to 127, each once within a row
- head_weight: bfloat16 [1024, 512], replicated, may hold values from -0.1875 to 0.1875
Outputs:
- grad_embeddings: bfloat16 [32768, 1024], P(('shuf', 'key'))
- grad_head: float32 [1024, 512], P('key')
The draws below stay inside these ranges and needn't reach their ends.
All inputs are finite; a program needn't handle non-finite values.
Results may differ from the reference program's by a relative error of at most 0.0075.
Values may be sent and summed in bfloat16 or wider, within the bound.
No kernel may reach another device: no remote copies, remote signals or barrier semaphores. Data moves between devices by JAX's collectives and lax.ppermute only.
A program may use at most 64 MiB of HBM per device.

```python
import jax
import jax.numpy as jnp
from jax import lax

D = 1024
PROJ = 512
ROWS = 128
BATCH = 32768
CLASSES = 2048
N_SHUF = 4
N_KEY = 64


def label_helper(key):
    return jax.random.randint(jax.random.fold_in(key, 11), (BATCH,), 0, CLASSES, dtype=jnp.int32)


def draw_labels(key, part):
    return label_helper(key)


def center_helper(key):
    family_count = max(CLASSES // 16, 1)
    family_of = jax.random.randint(jax.random.fold_in(key, 41), (CLASSES,), 0, family_count, dtype=jnp.int32)
    family_centers = jax.random.normal(jax.random.fold_in(key, 43), (family_count, D), jnp.float32)
    own_centers = jax.random.normal(jax.random.fold_in(key, 23), (CLASSES, D), jnp.float32)
    return 0.92 * family_centers[family_of] + 0.39 * own_centers


def draw_embeddings(key, part):
    class_ids = label_helper(key)
    centers = center_helper(key)
    noise = jax.random.normal(jax.random.fold_in(key, 29), (BATCH, D), jnp.float32)
    value = 1.5 * centers[class_ids] + noise
    value = jnp.clip(value, -200.0, 200.0)
    return value.astype(jnp.bfloat16)


def gaussian(rng, dims, deviation, reach, kind=jnp.bfloat16):
    values = deviation * jax.random.normal(rng, dims, jnp.float32)
    return jnp.clip(values, min=-reach, max=reach).astype(kind)


def setup_inputs(seed: int = 0) -> dict:
    streams_of = jax.random.split(jax.random.key(seed), 5)
    return {
        "embeddings": draw_embeddings(jax.random.fold_in(streams_of[4], 71), 0),
        "labels": draw_labels(jax.random.fold_in(streams_of[4], 71), 0),
        "order": jax.vmap(lambda own: jax.random.permutation(own, ROWS))(jax.random.split(streams_of[2], (N_SHUF * N_KEY))).reshape((N_SHUF * N_KEY, ROWS)).astype(jnp.int32),
        "head_weight": gaussian(streams_of[3], (D, PROJ), D ** -0.5, 0.1875),
    }


exponent_divisor = 0.1
loss_scale = 64.0
epsilon = 1e-06

def tile_terms(query_embeddings, anchor_labels, anchor_index, candidate_table, key_labels):
    cosine_score_table = lax.dot_general(query_embeddings, candidate_table, (((1,), (1,)), ((), ())), preferred_element_type=jnp.float32) / exponent_divisor
    column = jnp.arange(candidate_table.shape[0], dtype=jnp.int32)
    itself = anchor_index[:, None] == column[None, :]
    exponent = jnp.where(itself, 0.0, jnp.exp(cosine_score_table))
    positive = jnp.logical_and(anchor_labels[:, None] == key_labels[None, :], jnp.logical_not(itself)).astype(jnp.float32)
    return (exponent, positive)

def group_terms(grouped, group_labels, head_weight):
    projected = jnp.dot(grouped, head_weight, preferred_element_type=jnp.float32)
    row_norm = jnp.sqrt(lax.optimization_barrier(jnp.sum(projected * projected, axis=1, keepdims=True)) + epsilon)
    direction = projected / row_norm
    normed = direction.astype(jnp.bfloat16)
    cohort_extent = grouped.shape[0]
    block_count = cohort_extent // ROWS
    tile_starting_positions = jnp.arange(block_count, dtype=jnp.int32) * ROWS

    def first_block(offset):
        query_embeddings = lax.dynamic_slice_in_dim(normed, offset, ROWS, 0)
        anchor_labels = lax.dynamic_slice_in_dim(group_labels, offset, ROWS, 0)
        anchor_index = offset + jnp.arange(ROWS, dtype=jnp.int32)
        exponent, positive = tile_terms(query_embeddings, anchor_labels, anchor_index, normed, group_labels)
        return (lax.optimization_barrier(jnp.sum(exponent, axis=1)), lax.optimization_barrier(jnp.sum(positive, axis=1)))
    totals, counts = lax.map(first_block, tile_starting_positions)
    totals = totals.reshape(-1)
    counts = counts.reshape(-1)
    floor_count = jnp.maximum(counts, 1.0)
    soft_weight = loss_scale * counts / (floor_count * totals)
    pos_weight = loss_scale / floor_count

    def following_tile(offset):
        query_embeddings = lax.dynamic_slice_in_dim(normed, offset, ROWS, 0)
        anchor_labels = lax.dynamic_slice_in_dim(group_labels, offset, ROWS, 0)
        anchor_index = offset + jnp.arange(ROWS, dtype=jnp.int32)
        anchor_soft = lax.dynamic_slice_in_dim(soft_weight, offset, ROWS, 0)
        anchor_pos = lax.dynamic_slice_in_dim(pos_weight, offset, ROWS, 0)
        exponent, positive = tile_terms(query_embeddings, anchor_labels, anchor_index, normed, group_labels)
        coefficient = ((anchor_soft[:, None] + soft_weight[None, :]) * exponent - (anchor_pos[:, None] + pos_weight[None, :]) * positive).astype(jnp.bfloat16)
        return jnp.dot(coefficient, normed, preferred_element_type=jnp.float32)
    positive_pull_derivative = lax.map(following_tile, tile_starting_positions).reshape(cohort_extent, -1) / exponent_divisor
    along = lax.optimization_barrier(jnp.sum(direction * positive_pull_derivative, axis=1, keepdims=True))
    slopes = ((positive_pull_derivative - direction * along) / row_norm).astype(jnp.bfloat16)
    grad_rows = lax.dot_general(slopes, head_weight, (((1,), (1,)), ((), ())), preferred_element_type=jnp.float32).astype(jnp.bfloat16)
    head_part = lax.dot_general(grouped, slopes, (((0,), (0,)), ((), ())), preferred_element_type=jnp.float32)
    return (grad_rows, head_part)

def reference(embeddings, labels, order, head_weight):
    share_rows = ROWS // N_SHUF
    group_ids = jnp.arange(N_SHUF, dtype=jnp.int32)[:, None, None, None]
    key_ids = jnp.arange(N_KEY, dtype=jnp.int32)[None, :, None, None]
    source_ids = jnp.arange(N_SHUF, dtype=jnp.int32)[None, None, :, None]
    slot_ids = jnp.arange(share_rows, dtype=jnp.int32)[None, None, None, :]
    device_ids = source_ids * N_KEY + key_ids
    local_rows = order[device_ids, group_ids * share_rows + slot_ids]
    loader_rows = (device_ids * ROWS + local_rows).reshape(N_SHUF, N_KEY * ROWS).astype(jnp.int32)
    grad_embeddings = jnp.zeros_like(embeddings)
    grad_head = jnp.zeros((D, PROJ), jnp.float32)
    for group_id in range(N_SHUF):
        picked = loader_rows[group_id]
        grad_rows, head_part = group_terms(embeddings[picked], labels[picked], head_weight)
        grad_embeddings = grad_embeddings.at[picked].set(grad_rows)
        grad_head = grad_head + head_part
    return (grad_embeddings, grad_head / loss_scale)
```

```python
import jax
import jax.numpy as jnp
from jax import lax
from jax.sharding import Mesh, PartitionSpec as P

exponent_divisor = 0.1
loss_scale = 64.0
epsilon = 1e-06

AXES = ("yl", "c", "x", "zh", "zl", "yh")
KEY = ("x", "zh", "zl", "yh")
LABEL_ROWS = 16
f32 = jnp.float32
bf16 = jnp.bfloat16


def shift(value, axis, size, distance):
    distance %= size
    if distance == 0:
        return value
    return lax.ppermute(value, axis, [(i, (i + distance) % size) for i in range(size)])


def shift_y(value, distance):
    if distance % 4 == 0:
        return value
    seat = [(y % 2) * 2 + y // 2 for y in range(4)]
    return lax.ppermute(
        value, ("yl", "yh"), [(seat[y], seat[(y + distance) % 4]) for y in range(4)]
    )


def shift_yz(value, distance_y, distance_z):
    if distance_y == 0 and distance_z == 0:
        return value
    seat = lambda y, z: (y % 2) * 4 + z * 2 + y // 2
    pairs = [
        (seat(y, z), seat((y + distance_y) % 4, (z + distance_z) % 2))
        for y in range(4)
        for z in range(2)
    ]
    return lax.ppermute(value, ("yl", "zl", "yh"), pairs)


def unpack(stack, rows):
    normed = stack[:, :rows].reshape(-1, stack.shape[2])
    high = stack[:, rows, :rows].astype(jnp.int32)
    low = stack[:, rows, rows : 2 * rows].astype(jnp.int32)
    return normed, (high * 64 + low).reshape(-1)


def body(embeddings, labels, order, head_weight):
    rows, width = embeddings.shape
    proj = head_weight.shape[1]
    zh = lax.axis_index("zh")
    share = rows // 4
    doubled = jnp.concatenate([order[0], order[0]])
    routing = lax.dynamic_slice_in_dim(doubled, zh * share, rows)
    with jax.named_scope("route_out"):
        pick = (routing[:, None] == jnp.arange(rows, dtype=jnp.int32)[None, :]).astype(bf16)
        lane = jnp.arange(128, dtype=jnp.int32)[None, :]
        tag = jnp.where(
            lane == 0, (labels // 64)[:, None], jnp.where(lane == 1, (labels % 64)[:, None], 0)
        ).astype(bf16)
        tagged = jnp.concatenate([embeddings, tag], axis=1)
        sent = jnp.dot(pick, tagged, preferred_element_type=f32).astype(bf16)
        sent = sent.reshape(4, share, width + 128)
        got = jnp.concatenate([shift(sent[d], "zh", 4, d) for d in range(4)], axis=0)
    group_rows = got[:, :width]
    with jax.named_scope("project"):
        projected = jnp.dot(group_rows, head_weight, preferred_element_type=f32)
        row_norm = jnp.sqrt(jnp.sum(projected * projected, axis=1, keepdims=True) + epsilon)
        direction = projected / row_norm
        normed = direction.astype(bf16)
        label_line = jnp.concatenate(
            [got[:, width], got[:, width + 1], jnp.zeros((proj - 2 * rows,), bf16)]
        )
        label_block = jnp.broadcast_to(label_line[None, :], (LABEL_ROWS, proj))
        packet = jnp.concatenate([normed, label_block], axis=0)
    with jax.named_scope("gather_sets"):
        across_x = jnp.stack([shift(packet, "x", 4, d) for d in range(4)])
        set_b = jnp.stack([shift_yz(packet, dy, dz) for dy in range(4) for dz in range(2)])
        set_a = jnp.concatenate([across_x, shift(across_x, "c", 2, 1)], axis=0)
        normed_a, labels_a = unpack(set_a, rows)
        normed_b, labels_b = unpack(set_b, rows)
        chip_rows = lax.all_gather(group_rows, "c", axis=0, tiled=True)
    with jax.named_scope("scores"):
        total = normed_a.shape[0]
        scores = (
            lax.dot_general(
                normed_a, normed_b, (((1,), (1,)), ((), ())), preferred_element_type=f32
            )
            / exponent_divisor
        )
        row = jnp.arange(total, dtype=jnp.int32)
        itself = jnp.logical_and(row[:, None] == row[None, :], (row < rows)[:, None])
        exponent = jnp.where(itself, 0.0, jnp.exp(scores))
        positive = jnp.logical_and(
            labels_a[:, None] == labels_b[None, :], jnp.logical_not(itself)
        ).astype(f32)
        sums_a = jnp.stack([jnp.sum(exponent, axis=1), jnp.sum(positive, axis=1)])
        sums_b = jnp.stack([jnp.sum(exponent, axis=0), jnp.sum(positive, axis=0)])
    with jax.named_scope("totals"):
        sums_a = sums_a.reshape(2, 2, 4, rows)
        sums_a = sums_a + jnp.roll(shift(sums_a, "c", 2, 1), 1, axis=1)
        sums_a = sum([jnp.roll(shift(sums_a, "x", 4, d), d, axis=2) for d in range(4)])
        sums_b = sums_b.reshape(2, 4, 2, rows)
        sums_b = sums_b + jnp.roll(shift(sums_b, "zl", 2, 1), 1, axis=2)
        sums_b = sum([jnp.roll(shift_y(sums_b, d), d, axis=1) for d in range(4)])

        def weights(sums):
            totals, counts = sums.reshape(2, total)
            floor_count = jnp.maximum(counts, 1.0)
            return loss_scale * counts / (floor_count * totals), loss_scale / floor_count

        soft_a, pos_a = weights(sums_a)
        soft_b, pos_b = weights(sums_b)
    with jax.named_scope("pull"):
        coefficient = (
            (soft_a[:, None] + soft_b[None, :]) * exponent
            - (pos_a[:, None] + pos_b[None, :]) * positive
        ).astype(bf16)
        pull = jnp.dot(coefficient, normed_b, preferred_element_type=f32)
        pull = pull.reshape(2, 4, rows, proj)
        pull = pull[0] + shift(pull[1], "c", 2, 1)
        parts = [shift(pull[d].astype(bf16), "x", 4, -d).astype(f32) for d in range(1, 4)]
        pull_grad = (pull[0] + sum(parts)) / exponent_divisor
    with jax.named_scope("slopes"):
        along = jnp.sum(direction * pull_grad, axis=1, keepdims=True)
        slopes = ((pull_grad - direction * along) / row_norm).astype(bf16)
    with jax.named_scope("route_back"):
        blocks = slopes.reshape(4, share, proj)
        returned = jnp.concatenate([shift(blocks[d], "zh", 4, -d) for d in range(4)], axis=0)
        own = lax.dot_general(
            pick, returned, (((0,), (0,)), ((), ())), preferred_element_type=f32
        ).astype(bf16)
        grad_embeddings = lax.dot_general(
            own, head_weight, (((1,), (1,)), ((), ())), preferred_element_type=f32
        ).astype(bf16)
    with jax.named_scope("head"):
        chip_slopes = lax.all_gather(slopes, "c", axis=0, tiled=True)
        part = lax.dot_general(
            chip_rows, chip_slopes, (((0,), (0,)), ((), ())), preferred_element_type=f32
        ).astype(bf16)
        part = part.reshape(64, 2, width // 128, proj)
        part = lax.dynamic_index_in_dim(part, lax.axis_index("c"), axis=1, keepdims=False)
        part = part.reshape(128, width // 256, proj)
        spread = lax.all_to_all(part, KEY + ("yl",), split_axis=0, concat_axis=0, tiled=True)
        piece = jnp.sum(spread.astype(f32), axis=0)
        grad_head = lax.all_gather(piece, ("c", "yl"), axis=0, tiled=True)
    return (grad_embeddings, grad_head / loss_scale)


def solution(mesh):
    split = Mesh(mesh.devices.reshape(2, 2, 4, 4, 2, 2), AXES)
    return jax.shard_map(
        body,
        mesh=split,
        in_specs=(P(AXES, None), P(AXES), P(AXES, None), P()),
        out_specs=(P(AXES, None), P(KEY, None)),
        check_vma=False,
    )
```

```python
import jax
import jax.numpy as jnp
from jax import lax
from jax.sharding import Mesh, PartitionSpec as P

exponent_divisor = 0.1
loss_scale = 64.0
epsilon = 1e-06

AXES = ("yl", "c", "x", "zh", "zl", "yh")
KEY = ("x", "zh", "zl", "yh")
LABEL_ROWS = 16
f32 = jnp.float32
bf16 = jnp.bfloat16


def shift(value, axis, size, distance):
    distance %= size
    if distance == 0:
        return value
    return lax.ppermute(value, axis, [(i, (i + distance) % size) for i in range(size)])


def shift_y(value, distance):
    if distance % 4 == 0:
        return value
    seat = [(y % 2) * 2 + y // 2 for y in range(4)]
    return lax.ppermute(
        value, ("yl", "yh"), [(seat[y], seat[(y + distance) % 4]) for y in range(4)]
    )


def shift_yz(value, distance_y, distance_z):
    if distance_y == 0 and distance_z == 0:
        return value
    seat = lambda y, z: (y % 2) * 4 + z * 2 + y // 2
    pairs = [
        (seat(y, z), seat((y + distance_y) % 4, (z + distance_z) % 2))
        for y in range(4)
        for z in range(2)
    ]
    return lax.ppermute(value, ("yl", "zl", "yh"), pairs)


def unpack(stack, rows):
    normed = stack[:, :rows].reshape(-1, stack.shape[2])
    high = stack[:, rows, :rows].astype(jnp.int32)
    low = stack[:, rows, rows : 2 * rows].astype(jnp.int32)
    return normed, (high * 64 + low).reshape(-1)


def body(embeddings, labels, order, head_weight):
    rows, width = embeddings.shape
    proj = head_weight.shape[1]
    zh = lax.axis_index("zh")
    share = rows // 4
    doubled = jnp.concatenate([order[0], order[0]])
    routing = lax.dynamic_slice_in_dim(doubled, zh * share, rows)
    with jax.named_scope("route_out"):
        pick = (routing[:, None] == jnp.arange(rows, dtype=jnp.int32)[None, :]).astype(bf16)
        lane = jnp.arange(128, dtype=jnp.int32)[None, :]
        tag = jnp.where(
            lane == 0, (labels // 64)[:, None], jnp.where(lane == 1, (labels % 64)[:, None], 0)
        ).astype(bf16)
        tagged = jnp.concatenate([embeddings, tag], axis=1)
        sent = jnp.dot(pick, tagged, preferred_element_type=f32).astype(bf16)
        sent = sent.reshape(4, share, width + 128)
        got = jnp.concatenate([shift(sent[d], "zh", 4, d) for d in range(4)], axis=0)
    group_rows = got[:, :width]
    with jax.named_scope("project"):
        projected = jnp.dot(group_rows, head_weight, preferred_element_type=f32)
        row_norm = jnp.sqrt(jnp.sum(projected * projected, axis=1, keepdims=True) + epsilon)
        direction = projected / row_norm
        normed = direction.astype(bf16)
        label_line = jnp.concatenate(
            [got[:, width], got[:, width + 1], jnp.zeros((proj - 2 * rows,), bf16)]
        )
        label_block = jnp.broadcast_to(label_line[None, :], (LABEL_ROWS, proj))
        packet = jnp.concatenate([normed, label_block], axis=0)
    with jax.named_scope("gather_sets"):
        across_x = jnp.stack([shift(packet, "x", 4, d) for d in range(4)])
        set_b = jnp.stack([shift_yz(packet, dy, dz) for dy in range(4) for dz in range(2)])
        set_a = jnp.concatenate([across_x, shift(across_x, "c", 2, 1)], axis=0)
        normed_a, labels_a = unpack(set_a, rows)
        normed_b, labels_b = unpack(set_b, rows)
        chip_rows = lax.all_gather(group_rows, "c", axis=0, tiled=True)
    with jax.named_scope("scores"):
        total = normed_a.shape[0]
        scores = (
            lax.dot_general(
                normed_a, normed_b, (((1,), (1,)), ((), ())), preferred_element_type=f32
            )
            / exponent_divisor
        )
        row = jnp.arange(total, dtype=jnp.int32)
        itself = jnp.logical_and(row[:, None] == row[None, :], (row < rows)[:, None])
        exponent = jnp.where(itself, 0.0, jnp.exp(scores))
        positive = jnp.logical_and(
            labels_a[:, None] == labels_b[None, :], jnp.logical_not(itself)
        ).astype(f32)
        sums_a = jnp.stack([jnp.sum(exponent, axis=1), jnp.sum(positive, axis=1)])
        sums_b = jnp.stack([jnp.sum(exponent, axis=0), jnp.sum(positive, axis=0)])
    with jax.named_scope("totals"):
        sums_a = sums_a.reshape(2, 2, 4, rows)
        sums_a = sums_a + jnp.roll(shift(sums_a, "c", 2, 1), 1, axis=1)
        sums_a = sum([jnp.roll(shift(sums_a, "x", 4, d), d, axis=2) for d in range(4)])
        sums_b = sums_b.reshape(2, 4, 2, rows)
        sums_b = sums_b + jnp.roll(shift(sums_b, "zl", 2, 1), 1, axis=2)
        sums_b = sum([jnp.roll(shift_y(sums_b, d), d, axis=1) for d in range(4)])

        def weights(sums):
            totals, counts = sums.reshape(2, total)
            floor_count = jnp.maximum(counts, 1.0)
            return loss_scale * counts / (floor_count * totals), loss_scale / floor_count

        soft_a, pos_a = weights(sums_a)
        soft_b, pos_b = weights(sums_b)
    with jax.named_scope("pull"):
        coefficient = (
            (soft_a[:, None] + soft_b[None, :]) * exponent
            - (pos_a[:, None] + pos_b[None, :]) * positive
        ).astype(bf16)
        pull = jnp.dot(coefficient, normed_b, preferred_element_type=f32)
        pull = pull.reshape(2, 4, rows, proj)
        pull = pull[0] + shift(pull[1], "c", 2, 1)
        parts = [shift(pull[d].astype(bf16), "x", 4, -d).astype(f32) for d in range(1, 4)]
        pull_grad = (pull[0] + sum(parts)) / exponent_divisor
    with jax.named_scope("slopes"):
        along = jnp.sum(direction * pull_grad, axis=1, keepdims=True)
        slopes = ((pull_grad - direction * along) / row_norm).astype(bf16)
    with jax.named_scope("head_part"):
        blocks = slopes.reshape(4, share, proj)
        returned = [shift(blocks[d], "zh", 4, -d) for d in range(4)]
        chip_slopes = lax.all_gather(slopes, "c", axis=0, tiled=True)
        part = lax.dot_general(
            chip_rows, chip_slopes, (((0,), (0,)), ((), ())), preferred_element_type=f32
        ).astype(bf16)
        part = part.reshape(64, 2, width // 128, proj)
        part = lax.dynamic_index_in_dim(part, lax.axis_index("c"), axis=1, keepdims=False)
        part = part.reshape(128, width // 256, proj)
        part, *returned = lax.optimization_barrier((part, *returned))
    with jax.named_scope("head"):
        spread = lax.all_to_all(part, KEY + ("yl",), split_axis=0, concat_axis=0, tiled=True)
        piece = jnp.sum(spread.astype(f32), axis=0)
        other = shift(piece, "yl", 2, 1)
        first = lax.axis_index("yl") == 0
        pair = jnp.concatenate([jnp.where(first, piece, other), jnp.where(first, other, piece)])
        grad_head = lax.all_gather(pair, "c", axis=0, tiled=True)
    with jax.named_scope("route_back"):
        own = lax.dot_general(
            pick,
            jnp.concatenate(returned, axis=0),
            (((0,), (0,)), ((), ())),
            preferred_element_type=f32,
        ).astype(bf16)
        grad_embeddings = lax.dot_general(
            own, head_weight, (((1,), (1,)), ((), ())), preferred_element_type=f32
        ).astype(bf16)
    return (grad_embeddings, grad_head / loss_scale)


def solution(mesh):
    split = Mesh(mesh.devices.reshape(2, 2, 4, 4, 2, 2), AXES)
    return jax.shard_map(
        body,
        mesh=split,
        in_specs=(P(AXES, None), P(AXES), P(AXES, None), P()),
        out_specs=(P(AXES, None), P(KEY, None)),
        check_vma=False,
    )
```

```python
import jax
import jax.numpy as jnp
from jax import lax
from jax.sharding import Mesh, PartitionSpec as P

exponent_divisor = 0.1
loss_scale = 64.0
epsilon = 1e-06

AXES = ("yl", "c", "x", "zh", "zl", "yh")
KEY = ("x", "zh", "zl", "yh")
LABEL_ROWS = 16
f32 = jnp.float32
bf16 = jnp.bfloat16


def shift(value, axis, size, distance):
    distance %= size
    if distance == 0:
        return value
    return lax.ppermute(value, axis, [(i, (i + distance) % size) for i in range(size)])


def shift_y(value, distance):
    if distance % 4 == 0:
        return value
    seat = [(y % 2) * 2 + y // 2 for y in range(4)]
    return lax.ppermute(
        value, ("yl", "yh"), [(seat[y], seat[(y + distance) % 4]) for y in range(4)]
    )


def unpack(stack, rows):
    normed = stack[:, :rows].reshape(-1, stack.shape[2])
    high = stack[:, rows, :rows].astype(jnp.int32)
    low = stack[:, rows, rows : 2 * rows].astype(jnp.int32)
    return normed, (high * 64 + low).reshape(-1)


def body(embeddings, labels, order, head_weight):
    rows, width = embeddings.shape
    proj = head_weight.shape[1]
    zh = lax.axis_index("zh")
    share = rows // 4
    doubled = jnp.concatenate([order[0], order[0]])
    routing = lax.dynamic_slice_in_dim(doubled, zh * share, rows)
    with jax.named_scope("route_out"):
        pick = (routing[:, None] == jnp.arange(rows, dtype=jnp.int32)[None, :]).astype(bf16)
        lane = jnp.arange(128, dtype=jnp.int32)[None, :]
        tag = jnp.where(
            lane == 0, (labels // 64)[:, None], jnp.where(lane == 1, (labels % 64)[:, None], 0)
        ).astype(bf16)
        tagged = jnp.concatenate([embeddings, tag], axis=1)
        sent = jnp.dot(pick, tagged, preferred_element_type=f32).astype(bf16)
        sent = sent.reshape(4, share, width + 128)
        got = jnp.concatenate([shift(sent[d], "zh", 4, d) for d in range(4)], axis=0)
    group_rows = got[:, :width]
    with jax.named_scope("project"):
        projected = jnp.dot(group_rows, head_weight, preferred_element_type=f32)
        row_norm = jnp.sqrt(jnp.sum(projected * projected, axis=1, keepdims=True) + epsilon)
        direction = projected / row_norm
        normed = direction.astype(bf16)
        label_line = jnp.concatenate(
            [got[:, width], got[:, width + 1], jnp.zeros((proj - 2 * rows,), bf16)]
        )
        label_block = jnp.broadcast_to(label_line[None, :], (LABEL_ROWS, proj))
        packet = jnp.concatenate([normed, label_block], axis=0)
    with jax.named_scope("gather_sets"):
        across_x = jnp.stack([shift(packet, "x", 4, d) for d in range(4)])
        across_y = [shift_y(packet, d) for d in range(4)]
        set_b = jnp.stack([shift(block, "zl", 2, dz) for block in across_y for dz in range(2)])
        set_a = jnp.concatenate([across_x, shift(across_x, "c", 2, 1)], axis=0)
        normed_a, labels_a = unpack(set_a, rows)
        normed_b, labels_b = unpack(set_b, rows)
        chip_rows = lax.all_gather(group_rows, "c", axis=0, tiled=True)
    with jax.named_scope("scores"):
        total = normed_a.shape[0]
        scores = (
            lax.dot_general(
                normed_a, normed_b, (((1,), (1,)), ((), ())), preferred_element_type=f32
            )
            / exponent_divisor
        )
        row = jnp.arange(total, dtype=jnp.int32)
        itself = jnp.logical_and(row[:, None] == row[None, :], (row < rows)[:, None])
        exponent = jnp.where(itself, 0.0, jnp.exp(scores))
        positive = jnp.logical_and(
            labels_a[:, None] == labels_b[None, :], jnp.logical_not(itself)
        ).astype(f32)
        sums_a = jnp.stack([jnp.sum(exponent, axis=1), jnp.sum(positive, axis=1)])
        sums_b = jnp.stack([jnp.sum(exponent, axis=0), jnp.sum(positive, axis=0)])
    with jax.named_scope("totals"):
        sums_a = sums_a.reshape(2, 2, 4, rows)
        sums_a = sums_a + jnp.roll(shift(sums_a, "c", 2, 1), 1, axis=1)
        sums_a = sum([jnp.roll(shift(sums_a, "x", 4, d), d, axis=2) for d in range(4)])
        sums_b = sums_b.reshape(2, 4, 2, rows)
        sums_b = sums_b + jnp.roll(shift(sums_b, "zl", 2, 1), 1, axis=2)
        sums_b = sum([jnp.roll(shift_y(sums_b, d), d, axis=1) for d in range(4)])

        def weights(sums):
            totals, counts = sums.reshape(2, total)
            floor_count = jnp.maximum(counts, 1.0)
            return loss_scale * counts / (floor_count * totals), loss_scale / floor_count

        soft_a, pos_a = weights(sums_a)
        soft_b, pos_b = weights(sums_b)
    with jax.named_scope("pull"):
        half = total // 2

        def pull_rows(start):
            take = slice(start, start + half)
            coefficient = (
                (soft_a[take, None] + soft_b[None, :]) * exponent[take]
                - (pos_a[take, None] + pos_b[None, :]) * positive[take]
            ).astype(bf16)
            part = jnp.dot(coefficient, normed_b, preferred_element_type=f32)
            return part.reshape(4, rows, proj)

        crossing = shift(pull_rows(half), "c", 2, 1)
        pull = lax.optimization_barrier(pull_rows(0)) + crossing
        parts = [shift(pull[d].astype(bf16), "x", 4, -d).astype(f32) for d in range(1, 4)]
        pull_grad = (pull[0] + sum(parts)) / exponent_divisor
    with jax.named_scope("slopes"):
        along = jnp.sum(direction * pull_grad, axis=1, keepdims=True)
        slopes = ((pull_grad - direction * along) / row_norm).astype(bf16)
    with jax.named_scope("route_back"):
        blocks = slopes.reshape(4, share, proj)
        returned = jnp.concatenate([shift(blocks[d], "zh", 4, -d) for d in range(4)], axis=0)
        own = lax.dot_general(
            pick, returned, (((0,), (0,)), ((), ())), preferred_element_type=f32
        ).astype(bf16)
        grad_embeddings = lax.dot_general(
            own, head_weight, (((1,), (1,)), ((), ())), preferred_element_type=f32
        ).astype(bf16)
    with jax.named_scope("head"):
        chip_slopes = lax.all_gather(slopes, "c", axis=0, tiled=True)
        part = lax.dot_general(
            chip_rows, chip_slopes, (((0,), (0,)), ((), ())), preferred_element_type=f32
        ).astype(bf16)
        part = part.reshape(64, 2, width // 128, proj)
        part = lax.dynamic_index_in_dim(part, lax.axis_index("c"), axis=1, keepdims=False)
        spread = lax.all_to_all(part, KEY, split_axis=0, concat_axis=0, tiled=True)
        piece = jnp.sum(spread.astype(f32), axis=0)
        piece = piece + shift(piece, "yl", 2, 1)
        grad_head = lax.all_gather(piece, "c", axis=0, tiled=True)
    return (grad_embeddings, grad_head / loss_scale)


def solution(mesh):
    split = Mesh(mesh.devices.reshape(2, 2, 4, 4, 2, 2), AXES)
    return jax.shard_map(
        body,
        mesh=split,
        in_specs=(P(AXES, None), P(AXES), P(AXES, None), P()),
        out_specs=(P(AXES, None), P(KEY, None)),
        check_vma=False,
    )
```

```python
import jax
import jax.numpy as jnp
from jax import lax
from jax.sharding import Mesh, PartitionSpec as P

exponent_divisor = 0.1
loss_scale = 64.0
epsilon = 1e-06

AXES = ("yl", "c", "x", "zh", "zl", "yh")
KEY = ("x", "zh", "zl", "yh")
LABEL_ROWS = 16
f32 = jnp.float32
bf16 = jnp.bfloat16


def shift(value, axis, size, distance):
    distance %= size
    if distance == 0:
        return value
    return lax.ppermute(value, axis, [(i, (i + distance) % size) for i in range(size)])


def shift_y(value, distance):
    if distance % 4 == 0:
        return value
    seat = [(y % 2) * 2 + y // 2 for y in range(4)]
    return lax.ppermute(
        value, ("yl", "yh"), [(seat[y], seat[(y + distance) % 4]) for y in range(4)]
    )


def unpack(stack, rows):
    normed = stack[:, :rows].reshape(-1, stack.shape[2])
    high = stack[:, rows, :rows].astype(jnp.int32)
    low = stack[:, rows, rows : 2 * rows].astype(jnp.int32)
    return normed, (high * 64 + low).reshape(-1)


def body(embeddings, labels, order, head_weight):
    rows, width = embeddings.shape
    proj = head_weight.shape[1]
    zh = lax.axis_index("zh")
    share = rows // 4
    doubled = jnp.concatenate([order[0], order[0]])
    routing = lax.dynamic_slice_in_dim(doubled, zh * share, rows)
    with jax.named_scope("route_out"):
        pick = (routing[:, None] == jnp.arange(rows, dtype=jnp.int32)[None, :]).astype(bf16)
        lane = jnp.arange(128, dtype=jnp.int32)[None, :]
        tag = jnp.where(
            lane == 0, (labels // 64)[:, None], jnp.where(lane == 1, (labels % 64)[:, None], 0)
        ).astype(bf16)
        tagged = jnp.concatenate([embeddings, tag], axis=1)
        sent = jnp.dot(pick, tagged, preferred_element_type=f32).astype(bf16)
        sent = sent.reshape(4, share, width + 128)
        got = jnp.concatenate([shift(sent[d], "zh", 4, d) for d in range(4)], axis=0)
    group_rows = got[:, :width]

    def project(values):
        projected = jnp.dot(values, head_weight, preferred_element_type=f32)
        norm = jnp.sqrt(jnp.sum(projected * projected, axis=1, keepdims=True) + epsilon)
        return projected / norm, norm

    with jax.named_scope("project"):
        direction, row_norm = project(group_rows)
        normed = direction.astype(bf16)
        label_line = jnp.concatenate(
            [got[:, width], got[:, width + 1], jnp.zeros((proj - 2 * rows,), bf16)]
        )
        label_block = jnp.broadcast_to(label_line[None, :], (LABEL_ROWS, proj))
        packet = jnp.concatenate([normed, label_block], axis=0)
    with jax.named_scope("gather_sets"):
        across_x = jnp.stack([shift(got, "x", 4, d) for d in range(4)])
        across_y = [shift_y(packet, d) for d in range(4)]
        set_b = jnp.stack([shift(block, "zl", 2, dz) for block in across_y for dz in range(2)])
        normed_b, labels_b = unpack(set_b, rows)
        set_a = jnp.concatenate([across_x, shift(across_x, "c", 2, 1)], axis=0)
        set_a = set_a.reshape(-1, width + 128)
        rows_a = set_a[:, :width]
        high = set_a[:, width].astype(jnp.int32)
        labels_a = high * 64 + set_a[:, width + 1].astype(jnp.int32)
        direction_a, norm_a = project(rows_a)
        normed_a = direction_a.astype(bf16)
    with jax.named_scope("scores"):
        total = normed_a.shape[0]
        scores = (
            lax.dot_general(
                normed_a, normed_b, (((1,), (1,)), ((), ())), preferred_element_type=f32
            )
            / exponent_divisor
        )
        row = jnp.arange(total, dtype=jnp.int32)
        itself = jnp.logical_and(row[:, None] == row[None, :], (row < rows)[:, None])
        exponent = jnp.where(itself, 0.0, jnp.exp(scores))
        positive = jnp.logical_and(
            labels_a[:, None] == labels_b[None, :], jnp.logical_not(itself)
        ).astype(f32)
        sums_a = jnp.stack([jnp.sum(exponent, axis=1), jnp.sum(positive, axis=1)])
        sums_b = jnp.stack([jnp.sum(exponent, axis=0), jnp.sum(positive, axis=0)])
    with jax.named_scope("totals"):
        sums_a = sums_a.reshape(2, 2, 4, rows)
        sums_a = sums_a + jnp.roll(shift(sums_a, "c", 2, 1), 1, axis=1)
        sums_a = sum([jnp.roll(shift(sums_a, "x", 4, d), d, axis=2) for d in range(4)])
        sums_b = sums_b.reshape(2, 4, 2, rows)
        sums_b = sums_b + jnp.roll(shift(sums_b, "zl", 2, 1), 1, axis=2)
        sums_b = sum([jnp.roll(shift_y(sums_b, d), d, axis=1) for d in range(4)])

        def weights(sums):
            totals, counts = sums.reshape(2, total)
            floor_count = jnp.maximum(counts, 1.0)
            return loss_scale * counts / (floor_count * totals), loss_scale / floor_count

        soft_a, pos_a = weights(sums_a)
        soft_b, pos_b = weights(sums_b)
    with jax.named_scope("pull"):
        half = total // 2

        def pull_rows(start):
            take = slice(start, start + half)
            coefficient = (
                (soft_a[take, None] + soft_b[None, :]) * exponent[take]
                - (pos_a[take, None] + pos_b[None, :]) * positive[take]
            ).astype(bf16)
            part = jnp.dot(coefficient, normed_b, preferred_element_type=f32)
            return part.reshape(4, rows, proj)

        pull_far = pull_rows(half)
        crossing = shift(pull_far, "c", 2, 1)
        pull_near = lax.optimization_barrier(pull_rows(0))

    def to_slopes(pull_grad, unit, norm):
        along = jnp.sum(unit * pull_grad, axis=1, keepdims=True)
        return ((pull_grad - unit * along) / norm).astype(bf16)

    with jax.named_scope("head"):
        pull_part = jnp.concatenate([pull_near, pull_far]).reshape(total, proj)
        slopes_part = to_slopes(pull_part / exponent_divisor, direction_a, norm_a)
        part = lax.dot_general(
            rows_a, slopes_part, (((0,), (0,)), ((), ())), preferred_element_type=f32
        )
        part = part.reshape(64, 2, width // 128, proj)
        core = lax.axis_index("c")
        kept = lax.dynamic_index_in_dim(part, core, axis=1, keepdims=False)
        given = lax.dynamic_index_in_dim(part, 1 - core, axis=1, keepdims=False)
        part = (kept + shift(given.astype(bf16), "c", 2, 1).astype(f32)).astype(bf16)
        spread = lax.all_to_all(part, KEY, split_axis=0, concat_axis=0, tiled=True)
        piece = jnp.sum(spread.astype(f32), axis=0)
        piece = piece + shift(piece, "yl", 2, 1)
        grad_head = lax.all_gather(piece, "c", axis=0, tiled=True)
    with jax.named_scope("slopes"):
        pull = pull_near + crossing
        parts = [shift(pull[d].astype(bf16), "x", 4, -d).astype(f32) for d in range(1, 4)]
        pull_grad = (pull[0] + sum(parts)) / exponent_divisor
        slopes = to_slopes(pull_grad, direction, row_norm)
    with jax.named_scope("route_back"):
        blocks = slopes.reshape(4, share, proj)
        returned = jnp.concatenate([shift(blocks[d], "zh", 4, -d) for d in range(4)], axis=0)
        own = lax.dot_general(
            pick, returned, (((0,), (0,)), ((), ())), preferred_element_type=f32
        ).astype(bf16)
        grad_embeddings = lax.dot_general(
            own, head_weight, (((1,), (1,)), ((), ())), preferred_element_type=f32
        ).astype(bf16)
    return (grad_embeddings, grad_head / loss_scale)


def solution(mesh):
    split = Mesh(mesh.devices.reshape(2, 2, 4, 4, 2, 2), AXES)
    return jax.shard_map(
        body,
        mesh=split,
        in_specs=(P(AXES, None), P(AXES), P(AXES, None), P()),
        out_specs=(P(AXES, None), P(KEY, None)),
        check_vma=False,
    )
```

```python
import jax
import jax.numpy as jnp
from jax import lax
from jax.sharding import Mesh, PartitionSpec as P

exponent_divisor = 0.1
loss_scale = 64.0
epsilon = 1e-06

AXES = ("yl", "c", "x", "zh", "zl", "yh")
KEY = ("x", "zh", "zl", "yh")
LABEL_ROWS = 16
f32 = jnp.float32
bf16 = jnp.bfloat16


def shift(value, axis, size, distance):
    distance %= size
    if distance == 0:
        return value
    return lax.ppermute(value, axis, [(i, (i + distance) % size) for i in range(size)])


def shift_y(value, distance):
    if distance % 4 == 0:
        return value
    seat = [(y % 2) * 2 + y // 2 for y in range(4)]
    return lax.ppermute(
        value, ("yl", "yh"), [(seat[y], seat[(y + distance) % 4]) for y in range(4)]
    )


def quad(value):
    other = shift(value, "yl", 2, 1)
    chips = [lax.all_gather(block, "c", axis=0, tiled=True) for block in (value, other)]
    return jnp.concatenate(chips, axis=0)


def unpack(stack, rows):
    normed = stack[:, :rows].reshape(-1, stack.shape[2])
    high = stack[:, rows, :rows].astype(jnp.int32)
    low = stack[:, rows, rows : 2 * rows].astype(jnp.int32)
    return normed, (high * 64 + low).reshape(-1)


def body(embeddings, labels, order, head_weight):
    rows, width = embeddings.shape
    proj = head_weight.shape[1]
    zh = lax.axis_index("zh")
    share = rows // 4
    doubled = jnp.concatenate([order[0], order[0]])
    routing = lax.dynamic_slice_in_dim(doubled, zh * share, rows)
    with jax.named_scope("route_out"):
        pick = (routing[:, None] == jnp.arange(rows, dtype=jnp.int32)[None, :]).astype(bf16)
        lane = jnp.arange(128, dtype=jnp.int32)[None, :]
        tag = jnp.where(
            lane == 0, (labels // 64)[:, None], jnp.where(lane == 1, (labels % 64)[:, None], 0)
        ).astype(bf16)
        tagged = jnp.concatenate([embeddings, tag], axis=1)
        sent = jnp.dot(pick, tagged, preferred_element_type=f32).astype(bf16)
        sent = sent.reshape(4, share, width + 128)
        got = jnp.concatenate([shift(sent[d], "zh", 4, d) for d in range(4)], axis=0)
    group_rows = got[:, :width]
    with jax.named_scope("project"):
        projected = jnp.dot(group_rows, head_weight, preferred_element_type=f32)
        row_norm = jnp.sqrt(jnp.sum(projected * projected, axis=1, keepdims=True) + epsilon)
        direction = projected / row_norm
        normed = direction.astype(bf16)
        label_line = jnp.concatenate(
            [got[:, width], got[:, width + 1], jnp.zeros((proj - 2 * rows,), bf16)]
        )
        label_block = jnp.broadcast_to(label_line[None, :], (LABEL_ROWS, proj))
        packet = jnp.concatenate([normed, label_block], axis=0)
    with jax.named_scope("gather_sets"):
        across_x = jnp.stack([shift(packet, "x", 4, d) for d in range(4)])
        across_y = [shift_y(packet, d) for d in range(4)]
        set_b = jnp.stack([shift(block, "zl", 2, dz) for block in across_y for dz in range(2)])
        set_a = jnp.concatenate([across_x, shift(across_x, "c", 2, 1)], axis=0)
        normed_a, labels_a = unpack(set_a, rows)
        normed_b, labels_b = unpack(set_b, rows)
        quad_rows = quad(group_rows)
    with jax.named_scope("scores"):
        total = normed_a.shape[0]
        scores = (
            lax.dot_general(
                normed_a, normed_b, (((1,), (1,)), ((), ())), preferred_element_type=f32
            )
            / exponent_divisor
        )
        row = jnp.arange(total, dtype=jnp.int32)
        itself = jnp.logical_and(row[:, None] == row[None, :], (row < rows)[:, None])
        exponent = jnp.where(itself, 0.0, jnp.exp(scores))
        positive = jnp.logical_and(
            labels_a[:, None] == labels_b[None, :], jnp.logical_not(itself)
        ).astype(f32)
        sums_a = jnp.stack([jnp.sum(exponent, axis=1), jnp.sum(positive, axis=1)])
        sums_b = jnp.stack([jnp.sum(exponent, axis=0), jnp.sum(positive, axis=0)])
    with jax.named_scope("totals"):
        sums_a = sums_a.reshape(2, 2, 4, rows)
        sums_a = sums_a + jnp.roll(shift(sums_a, "c", 2, 1), 1, axis=1)
        sums_a = sum([jnp.roll(shift(sums_a, "x", 4, d), d, axis=2) for d in range(4)])
        sums_b = sums_b.reshape(2, 4, 2, rows)
        sums_b = sums_b + jnp.roll(shift(sums_b, "zl", 2, 1), 1, axis=2)
        sums_b = sum([jnp.roll(shift_y(sums_b, d), d, axis=1) for d in range(4)])

        def weights(sums):
            totals, counts = sums.reshape(2, total)
            floor_count = jnp.maximum(counts, 1.0)
            return loss_scale * counts / (floor_count * totals), loss_scale / floor_count

        soft_a, pos_a = weights(sums_a)
        soft_b, pos_b = weights(sums_b)
    with jax.named_scope("pull"):
        half = total // 2

        def pull_rows(start):
            take = slice(start, start + half)
            coefficient = (
                (soft_a[take, None] + soft_b[None, :]) * exponent[take]
                - (pos_a[take, None] + pos_b[None, :]) * positive[take]
            ).astype(bf16)
            part = jnp.dot(coefficient, normed_b, preferred_element_type=f32)
            return part.reshape(4, rows, proj)

        crossing = shift(pull_rows(half), "c", 2, 1)
        pull = lax.optimization_barrier(pull_rows(0)) + crossing
        parts = [shift(pull[d].astype(bf16), "x", 4, -d).astype(f32) for d in range(1, 4)]
        pull_grad = (pull[0] + sum(parts)) / exponent_divisor
    with jax.named_scope("slopes"):
        along = jnp.sum(direction * pull_grad, axis=1, keepdims=True)
        slopes = ((pull_grad - direction * along) / row_norm).astype(bf16)
    with jax.named_scope("head"):
        blocks = slopes.reshape(4, share, proj)
        returned = [shift(blocks[d], "zh", 4, -d) for d in range(4)]
        quad_slopes = quad(slopes)
        part = lax.dot_general(
            quad_rows, quad_slopes, (((0,), (0,)), ((), ())), preferred_element_type=f32
        ).astype(bf16)
        part = part.reshape(64, 4, width // 256, proj)
        seat = 2 * lax.axis_index("c") + lax.axis_index("yl")
        part = lax.dynamic_index_in_dim(part, seat, axis=1, keepdims=False)
        part, returned[1], returned[3] = lax.optimization_barrier(
            (part, returned[1], returned[3])
        )
        spread = lax.all_to_all(part, KEY, split_axis=0, concat_axis=0, tiled=True)
        piece = jnp.sum(spread.astype(f32), axis=0)
        other = shift(piece, "yl", 2, 1)
        first = lax.axis_index("yl") == 0
        pair = jnp.concatenate([jnp.where(first, piece, other), jnp.where(first, other, piece)])
        grad_head = lax.all_gather(pair, "c", axis=0, tiled=True)
    with jax.named_scope("route_back"):
        own = lax.dot_general(
            pick,
            jnp.concatenate(returned, axis=0),
            (((0,), (0,)), ((), ())),
            preferred_element_type=f32,
        ).astype(bf16)
        grad_embeddings = lax.dot_general(
            own, head_weight, (((1,), (1,)), ((), ())), preferred_element_type=f32
        ).astype(bf16)
    return (grad_embeddings, grad_head / loss_scale)


def solution(mesh):
    split = Mesh(mesh.devices.reshape(2, 2, 4, 4, 2, 2), AXES)
    return jax.shard_map(
        body,
        mesh=split,
        in_specs=(P(AXES, None), P(AXES), P(AXES, None), P()),
        out_specs=(P(AXES, None), P(KEY, None)),
        check_vma=False,
    )
```
